32 devices in a mesh: rows: 4 (over x, core), seq: 8 (over z, y).
Axes of the slice: x: 2, y: 2, z: 4, core: 2. Of those that a mesh axis runs over, the one named last changes fastest.
Arguments:
- inputs: bfloat16 [8, 1024, 2048], P('rows', 'seq'), may hold values from -6 to 6
- cotangent: bfloat16 [8, 1024, 2048], P('rows', 'seq'), may hold values from -6 to 6
- positions: int32 [8, 1024], P('rows', 'seq'), may hold values from 0 to 4095, as said below
- segment_ids: int32 [8, 1024], P('rows', 'seq'), may hold values from 0 to 3, as said below
- w_query: bfloat16 [2048, 1280], P(('rows', 'seq')), may hold values from -0.125 to 0.125
- w_key: bfloat16 [2048, 320], P(('rows', 'seq')), may hold values from -0.125 to 0.125
- w_value: bfloat16 [2048, 320], P(('rows', 'seq')), may hold values from -0.125 to 0.125
- w_out: bfloat16 [1280, 2048], P(('rows', 'seq')), may hold values from -0.625 to 0.625
- w_gate: bfloat16 [2048, 6656], P('seq', 'rows'), may hold values from -0.125 to 0.125
- w_up: bfloat16 [2048, 6656], P('seq', 'rows'), may hold values from -0.125 to 0.125
- w_down: bfloat16 [6656, 2048], P('rows', 'seq'), may hold values from -0.078125 to 0.078125
- gain_attn: bfloat16 [2048], P(('rows', 'seq')), may hold values from 0.5 to 1.5
- gain_query: bfloat16 [64], replicated, may hold values from 0.099609375 to 1.8984375
- gain_key: bfloat16 [64], replicated, may hold values from 0.099609375 to 1.8984375
- gain_ffn: bfloat16 [2048], P(('rows', 'seq')), may hold values from 0.5 to 1.5
Outputs:
- output: bfloat16 [8, 1024, 2048], P('rows', 'seq')
- grad_inputs: float32 [8, 1024, 2048], P('rows', 'seq')
- grad_query: float32 [2048, 1280], P(('rows', 'seq'))
- grad_key: float32 [2048, 320], P(('rows', 'seq'))
- grad_value: float32 [2048, 320], P(('rows', 'seq'))
- grad_out: float32 [1280, 2048], P(('rows', 'seq'))
- grad_gate: float32 [2048, 6656], P('seq', 'rows')
- grad_up: float32 [2048, 6656], P('seq', 'rows')
- grad_down: float32 [6656, 2048], P('rows', 'seq')
- grad_gain_attn: float32 [2048], P(('rows', 'seq'))
- grad_gain_query: float32 [64], replicated
- grad_gain_key: float32 [64], replicated
- grad_gain_ffn: float32 [2048], P(('rows', 'seq'))
The draws below stay inside these ranges and needn't reach their ends.
Inputs may be any that keep to these rules, and one draw needn't show every extreme that they name: `segment_ids`: within a packed row the ids never fall, start at 0, and every row holds exactly 4 documents of one token or more. Inside a document the positions rise by one from token to token; each document starts at its own position.
All inputs are finite; a program needn't handle non-finite values.
Results may differ from the reference program's by a relative error of at most 0.02.
Values may be sent and summed in bfloat16 or wider, within the bound.
No kernel may reach another device: no remote copies, remote signals or barrier semaphores. Data moves between devices by JAX's collectives and lax.ppermute only.
A program may use at most 256 MiB of HBM per device.

```python
import jax
import jax.numpy as jnp
from jax import lax

D = 2048
FF = 6656
HQ = 20
HK = 5
HD = 64
NSEG = 4
POS_MAX = 4095
ROWS = 8
ROW_LEN = 1024


def packed_layout(key):
    base_key = jax.random.fold_in(key, 17)
    row_keys = jax.random.split(base_key, ROWS)
    index_row = jnp.arange(ROW_LEN, dtype=jnp.int32)
    last_slot = jnp.arange(NSEG, dtype=jnp.int32)

    def one_row(row_key, row_number):
        cut_key, shift_key = jax.random.split(row_key)
        picked = jax.random.permutation(cut_key, ROW_LEN - 1)[:NSEG - 1].astype(jnp.int32) + 1
        cut_points = jnp.sort(picked)
        segment = jnp.sum((index_row[:, None] >= cut_points[None, :]).astype(jnp.int32), axis=1)
        bounds = jnp.concatenate([jnp.zeros((1,), jnp.int32), cut_points, jnp.full((1,), ROW_LEN, jnp.int32)])
        starts = bounds[:-1]
        lengths = bounds[1:] - starts
        shifts = jax.random.randint(shift_key, (NSEG,), 0, POS_MAX + 2 - lengths).astype(jnp.int32)
        first_row = row_number == 0
        shifts = jnp.where(first_row & (last_slot == NSEG - 1), POS_MAX + 1 - lengths, shifts)
        shifts = jnp.where(first_row & (last_slot == 0), 0, shifts)
        position_row = index_row - starts[segment] + shifts[segment]
        return (segment.astype(jnp.int32), position_row.astype(jnp.int32))
    return jax.vmap(one_row)(row_keys, jnp.arange(ROWS, dtype=jnp.int32))


def draw_positions(key, part):
    return packed_layout(key)[1]


def draw_segment_ids(key, part):
    return packed_layout(key)[0]


def block_levels(own_key, shape, cuts, smallest, top_value):
    def one(position, shards_of):
        steps = jax.random.uniform(jax.random.fold_in(jax.random.fold_in(own_key, 6), position), (shards_of,), jnp.float32, smallest / len(cuts), top_value / len(cuts))
        return jnp.repeat(jnp.exp(steps), shape[position] // shards_of).reshape((-1,) + (1,) * (len(shape) - position - 1))

    gain = one(*cuts[0])
    for cut in cuts[1:]:
        gain = gain * one(*cut)
    return gain


def normal_values(rng, shape, deviation, limit, pieces=(), held_as=jnp.bfloat16):
    values = deviation * jax.random.normal(rng, shape, jnp.float32)
    if pieces:
        values = values * block_levels(rng, shape, pieces, -0.22, 0.18)
    return jnp.clip(values, -limit, limit).astype(held_as)


def setup_inputs(seed: int = 0) -> dict:
    arg_keys = jax.random.split(jax.random.key(seed), 16)
    return {
        "inputs": normal_values(arg_keys[0], (ROWS, ROW_LEN, D), 1.0, 6.0, ((0, 4), (1, 8))),
        "cotangent": normal_values(arg_keys[1], (ROWS, ROW_LEN, D), 1.0, 6.0, ((0, 4), (1, 8))),
        "positions": draw_positions(jax.random.fold_in(arg_keys[15], 71), 0),
        "segment_ids": draw_segment_ids(jax.random.fold_in(arg_keys[15], 71), 0),
        "w_query": normal_values(arg_keys[4], (D, HQ * HD), D ** -0.5, 0.125, ((0, 32),)),
        "w_key": normal_values(arg_keys[5], (D, HK * HD), D ** -0.5, 0.125, ((0, 32),)),
        "w_value": normal_values(arg_keys[6], (D, HK * HD), D ** -0.5, 0.125, ((0, 32),)),
        "w_out": normal_values(arg_keys[7], (HQ * HD, D), (HQ * HD // 16) ** -0.5, 0.625, ((0, 32),)),
        "w_gate": normal_values(arg_keys[8], (D, FF), D ** -0.5, 0.125, ((0, 8), (1, 4))),
        "w_up": normal_values(arg_keys[9], (D, FF), D ** -0.5, 0.125, ((0, 8), (1, 4))),
        "w_down": normal_values(arg_keys[10], (FF, D), FF ** -0.5, 0.078125, ((0, 4), (1, 8))),
        "gain_attn": jnp.clip(1.0 + 0.1 * jax.random.normal(arg_keys[11], (D,), jnp.float32), 0.5, 1.5).astype(jnp.bfloat16),
        "gain_query": jnp.clip(1.0 + 0.18 * jax.random.normal(arg_keys[12], (HD,), jnp.float32), 0.099609375, 1.8984375).astype(jnp.bfloat16),
        "gain_key": jnp.clip(1.0 + 0.18 * jax.random.normal(arg_keys[13], (HD,), jnp.float32), 0.099609375, 1.8984375).astype(jnp.bfloat16),
        "gain_ffn": jnp.clip(1.0 + 0.1 * jax.random.normal(arg_keys[14], (D,), jnp.float32), 0.5, 1.5).astype(jnp.bfloat16),
    }


norm_eps = 1e-06
masked_score = -1e+30
highest = lax.Precision.HIGHEST

@jax.custom_vjp
def low(v):
    return lax.optimization_barrier(v.astype(jnp.bfloat16)).astype(jnp.float32)

@jax.custom_vjp
def low_back(v):
    return v

def low_keep(v):
    return (low(v), None)

def low_pass(kept, grad):
    return (grad,)

def back_keep(v):
    return (v, None)

def back_low(kept, grad):
    return (low(grad),)
low.defvjp(low_keep, low_pass)
low_back.defvjp(back_keep, back_low)

def rms_apply(values, gain_vec):
    row_scale = lax.rsqrt(lax.optimization_barrier(jnp.mean(values * values, axis=-1, keepdims=True)) + norm_eps)
    return values * row_scale * gain_vec

def rotary_tables(positions, head_dim):
    half_dim = head_dim // 2
    frequencies = 10000.0 ** (-2.0 * jnp.arange(half_dim).astype(jnp.float32) / head_dim)
    angles = positions.astype(jnp.float32)[..., None] * frequencies
    angles = jnp.concatenate([angles, angles], axis=-1)
    return (jnp.cos(angles), jnp.sin(angles))

def rotate(values, cosine, sine):
    half_dim = values.shape[-1] // 2
    turned = jnp.concatenate([-values[..., half_dim:], values[..., :half_dim]], axis=-1)
    return values * cosine + turned * sine

def matmul(left, right):
    return jnp.dot(left, right, precision=highest, preferred_element_type=jnp.float32)

def attend(query_rot, key_rot, value_low, segment_ids):
    span_len = min(512, ROW_LEN)
    blocks_per_row = ROW_LEN // span_len
    grouping = HQ // HK
    query_blocks = query_rot.reshape(ROWS * blocks_per_row, span_len, HK, grouping, HD)
    key_spots = jnp.arange(ROW_LEN, dtype=jnp.int32)

    def one_block(block_number):
        row_number = block_number // blocks_per_row
        block_start = block_number % blocks_per_row * span_len
        queries = lax.dynamic_index_in_dim(query_blocks, block_number, 0, keepdims=False)
        keys_row = lax.dynamic_index_in_dim(key_rot, row_number, 0, keepdims=False)
        values_row = lax.dynamic_index_in_dim(value_low, row_number, 0, keepdims=False)
        segs_row = lax.dynamic_index_in_dim(segment_ids, row_number, 0, keepdims=False)
        segs_query = lax.dynamic_slice_in_dim(segs_row, block_start, span_len)
        query_spots = block_start + jnp.arange(span_len, dtype=jnp.int32)
        scores = jnp.einsum('qhgd,khd->hgqk', queries, keys_row, precision=highest) * HD ** (-0.5)
        scores = low_back(scores)
        allowed = (key_spots[None, :] <= query_spots[:, None]) & (segs_query[:, None] == segs_row[None, :])
        scores = jnp.where(allowed, scores, masked_score)
        shifted = jnp.exp(scores - lax.optimization_barrier(jnp.max(scores, axis=-1, keepdims=True)))
        probs_low = low(shifted / lax.optimization_barrier(jnp.sum(shifted, axis=-1, keepdims=True)))
        mixed_out = jnp.einsum('hgqk,khd->qhgd', probs_low, values_row, precision=highest)
        return mixed_out.reshape(span_len, HQ * HD)
    blocks = lax.map(jax.checkpoint(one_block), jnp.arange(ROWS * blocks_per_row, dtype=jnp.int32))
    return blocks.reshape(ROWS * ROW_LEN, HQ * HD)

def forward(inputs, w_query, w_key, w_value, w_out, w_gate, w_up, w_down, gain_attn, gain_query, gain_key, gain_ffn, cosine, sine, segment_ids):
    flat_in = inputs.reshape(ROWS * ROW_LEN, D)
    normed = low(rms_apply(flat_in, gain_attn))
    query_pre = low_back(matmul(normed, w_query))
    key_pre = low_back(matmul(normed, w_key))
    value_low = low(low_back(matmul(normed, w_value)))
    query_rot = low(rotate(rms_apply(query_pre.reshape(ROWS * ROW_LEN, HQ, HD), gain_query), cosine, sine))
    key_rot = low(rotate(rms_apply(key_pre.reshape(ROWS * ROW_LEN, HK, HD), gain_key), cosine, sine))
    attended = attend(query_rot.reshape(ROWS, ROW_LEN, HQ, HD), key_rot.reshape(ROWS, ROW_LEN, HK, HD), value_low.reshape(ROWS, ROW_LEN, HK, HD), segment_ids)
    attended = low(low_back(attended))
    middle = flat_in + low_back(matmul(attended, w_out))
    ffn_in = low(rms_apply(middle, gain_ffn))
    gate_val = low_back(matmul(ffn_in, w_gate))
    up_val = low_back(matmul(ffn_in, w_up))
    hidden = low(jax.nn.silu(gate_val) * up_val)
    output = middle + low_back(matmul(hidden, w_down))
    return output.reshape(ROWS, ROW_LEN, D)

def reference(inputs, cotangent, positions, segment_ids, w_query, w_key, w_value, w_out, w_gate, w_up, w_down, gain_attn, gain_query, gain_key, gain_ffn):
    cosine, sine = rotary_tables(positions, HD)
    cosine = cosine.reshape(ROWS * ROW_LEN, 1, HD)
    sine = sine.reshape(ROWS * ROW_LEN, 1, HD)
    params = tuple((item.astype(jnp.float32) for item in (w_query, w_key, w_value, w_out, w_gate, w_up, w_down, gain_attn, gain_query, gain_key, gain_ffn)))

    def layer(inputs_f, *weights):
        return forward(inputs_f, *weights, cosine, sine, segment_ids)
    output, pullback = jax.vjp(layer, inputs.astype(jnp.float32), *params)
    grads = pullback(cotangent.astype(jnp.float32))
    return (output.astype(jnp.bfloat16), grads[0], grads[1], grads[2], grads[3], grads[4], grads[5], grads[6], grads[7], grads[8], grads[9], grads[10], grads[11])
```

```python
import jax
import jax.numpy as jnp
from jax import lax
from jax.sharding import PartitionSpec as P

norm_eps = 1e-06
masked_score = -1e30


def rms_apply(values, gain_vec):
    row_scale = lax.rsqrt(jnp.mean(values * values, axis=-1, keepdims=True) + norm_eps)
    return values * row_scale * gain_vec


def rms_back(values, gain_vec, grad_in):
    row_scale = lax.rsqrt(jnp.mean(values * values, axis=-1, keepdims=True) + norm_eps)
    weighted = grad_in * gain_vec
    inner_sum = jnp.sum(weighted * values, axis=-1, keepdims=True)
    grad_values = (
        row_scale * weighted
        - values * (row_scale * row_scale * row_scale) * inner_sum / values.shape[-1]
    )
    return (grad_values, grad_in * values * row_scale)


def rotary_tables(positions, head_dim):
    half_dim = head_dim // 2
    frequencies = 10000.0 ** (-2.0 * jnp.arange(half_dim).astype(jnp.float32) / head_dim)
    angles = positions.astype(jnp.float32)[..., None] * frequencies
    angles = jnp.concatenate([angles, angles], axis=-1)
    return (jnp.cos(angles), jnp.sin(angles))


def rotate(values, cosine, sine):
    half_dim = values.shape[-1] // 2
    turned = jnp.concatenate([-values[..., half_dim:], values[..., :half_dim]], axis=-1)
    return values * cosine + turned * sine


def rotate_back(grad_in, cosine, sine):
    half_dim = grad_in.shape[-1] // 2
    moved_part = grad_in * sine
    turned = jnp.concatenate([moved_part[..., half_dim:], -moved_part[..., :half_dim]], axis=-1)
    return grad_in * cosine + turned


def times_transposed(left, right):
    return lax.dot_general(
        left, right, (((1,), (1,)), ((), ())), preferred_element_type=jnp.float32
    )


def transposed_times(left, right):
    return lax.dot_general(
        left, right, (((0,), (0,)), ((), ())), preferred_element_type=jnp.float32
    )


def ring_spot(place, ring_size):
    return jnp.where(place % 2 == 0, place // 2, ring_size - (place + 1) // 2)


def ring_place(spot, ring_size):
    spot = spot % ring_size
    return jnp.where(spot < ring_size // 2, 2 * spot, 2 * ring_size - 1 - 2 * spot)


def ring_pairs(ring_size):
    order = list(range(0, ring_size, 2)) + list(range(ring_size - 1, 0, -2))
    ahead = [(order[i], order[(i + 1) % ring_size]) for i in range(ring_size)]
    return (ahead, [(b, a) for a, b in ahead])


def halves(chunk, axis):
    size = chunk.shape[axis] // 2
    return (
        lax.slice_in_dim(chunk, 0, size, axis=axis),
        lax.slice_in_dim(chunk, size, 2 * size, axis=axis),
    )


def ring_gather(chunk, axis, split_axis):
    ring_size = lax.axis_size("seq")
    ahead, behind = ring_pairs(ring_size)
    place = lax.axis_index("seq")
    spot = ring_spot(place, ring_size)
    size = chunk.shape[axis]
    shape = list(chunk.shape)
    shape[axis] = size * ring_size
    whole = jnp.zeros(tuple(shape), chunk.dtype)

    def put(whole, part, source, offset=0):
        starts = [0] * part.ndim
        starts[axis] = source * size
        if offset:
            starts[split_axis] = starts[split_axis] + offset
        return lax.dynamic_update_slice(whole, part, starts)

    whole = put(whole, chunk, place)
    from_behind = from_ahead = chunk
    for step in range(1, ring_size // 2):
        from_behind = lax.ppermute(from_behind, "seq", ahead)
        from_ahead = lax.ppermute(from_ahead, "seq", behind)
        whole = put(whole, from_behind, ring_place(spot - step, ring_size))
        whole = put(whole, from_ahead, ring_place(spot + step, ring_size))
    low_half = lax.ppermute(halves(from_behind, split_axis)[0], "seq", ahead)
    high_half = lax.ppermute(halves(from_ahead, split_axis)[1], "seq", behind)
    source = ring_place(spot + ring_size // 2, ring_size)
    whole = put(whole, low_half, source)
    return put(whole, high_half, source, low_half.shape[split_axis])


def ring_scatter(full, axis, split_axis):
    ring_size = lax.axis_size("seq")
    ahead, behind = ring_pairs(ring_size)
    spot = ring_spot(lax.axis_index("seq"), ring_size)
    size = full.shape[axis] // ring_size

    def part(which, half):
        starts = [0] * full.ndim
        sizes = list(full.shape)
        sizes[axis] = size
        starts[axis] = ring_place(which, ring_size) * size
        sizes[split_axis] = sizes[split_axis] // 2
        starts[split_axis] = starts[split_axis] + half * sizes[split_axis]
        return lax.dynamic_slice(full, starts, sizes)

    sums = [part(spot - 1, 0).astype(jnp.bfloat16), part(spot + 1, 1).astype(jnp.bfloat16)]
    for step in range(1, ring_size):
        low_sum = lax.ppermute(sums[0], "seq", ahead).astype(jnp.float32)
        high_sum = lax.ppermute(sums[1], "seq", behind).astype(jnp.float32)
        low_sum = low_sum + part(spot - 1 - step, 0).astype(jnp.float32)
        high_sum = high_sum + part(spot + 1 + step, 1).astype(jnp.float32)
        sums = [low_sum.astype(jnp.bfloat16), high_sum.astype(jnp.bfloat16)]
    return jnp.concatenate([low_sum, high_sum], axis=split_axis)


def swap_rows(values, distance):
    count = lax.axis_size("rows")
    return lax.ppermute(values, "rows", [(i, i ^ distance) for i in range(count)])


def rows_gather(values):
    near = swap_rows(values, 1)
    far = swap_rows(values, 2)
    return [values, near, far, swap_rows(far, 1)]


def rows_scatter(blocks):
    first = swap_rows(blocks[3], 1).astype(jnp.float32)
    cross = swap_rows((first + blocks[2].astype(jnp.float32)).astype(jnp.bfloat16), 2)
    second = swap_rows(blocks[1], 1).astype(jnp.float32)
    return blocks[0].astype(jnp.float32) + second + cross.astype(jnp.float32)


def rows_order(blocks, axis):
    own = lax.axis_index("rows")
    size = blocks[0].shape[axis]
    shape = list(blocks[0].shape)
    shape[axis] = size * len(blocks)
    whole = jnp.zeros(tuple(shape), blocks[0].dtype)
    for distance, block in enumerate(blocks):
        starts = [0] * block.ndim
        starts[axis] = (own ^ distance) * size
        whole = lax.dynamic_update_slice(whole, block, starts)
    return whole


def rows_exchange(values):
    count = lax.axis_size("rows")
    own = lax.axis_index("rows")
    size = values.shape[1] // count
    parts = []
    for distance in range(count):
        part = lax.dynamic_slice_in_dim(values, (own ^ distance) * size, size, 1)
        parts.append(swap_rows(part, distance) if distance else part)
    return jnp.concatenate(parts, axis=0)


def local(
    inputs,
    cotangent,
    positions,
    segment_ids,
    w_query,
    w_key,
    w_value,
    w_out,
    w_gate,
    w_up,
    w_down,
    gain_attn,
    gain_query,
    gain_key,
    gain_ffn,
):
    rows_here, seg_tok, feature_count = inputs.shape
    tokens_here = rows_here * seg_tok
    head_dim = gain_query.shape[0]
    heads_query = w_query.shape[1] // head_dim
    heads_kv = w_key.shape[1] // head_dim
    grouping = heads_query // heads_kv
    row_len = seg_tok * lax.axis_size("seq")
    key_block = min(512, row_len)
    block_total = row_len // key_block
    score_scale = head_dim ** (-0.5)
    seq_place = lax.axis_index("seq")
    query_width = w_query.shape[1]
    kv_width = w_key.shape[1]
    attn_width = query_width + 2 * kv_width
    feature_share = w_query.shape[0]
    pad_width = -(attn_width + 2) % 128
    attn_shard = jnp.concatenate(
        [
            w_query,
            w_key,
            w_value,
            gain_attn[:, None],
            gain_ffn[:, None],
            jnp.zeros((feature_share, pad_width), jnp.bfloat16),
        ],
        axis=1,
    )
    attn_full = rows_order(rows_gather(ring_gather(attn_shard, 0, 0)), 0)
    out_full = rows_order(rows_gather(ring_gather(w_out, 0, 1)), 0)
    gate_loc = ring_gather(w_gate, 0, 0)
    up_loc = ring_gather(w_up, 0, 0)
    down_loc = ring_gather(w_down, 1, 0)
    seg_keys = lax.all_gather(segment_ids.astype(jnp.bfloat16), "seq", axis=1, tiled=True)
    gain_attn_full = attn_full[:, attn_width].astype(jnp.float32)
    gain_ffn_full = attn_full[:, attn_width + 1].astype(jnp.float32)
    grad_top_b = cotangent.reshape(tokens_here, feature_count)
    cot_all = jnp.concatenate(rows_gather(grad_top_b), axis=0)
    residual = inputs.astype(jnp.float32).reshape(tokens_here, feature_count)
    normed = rms_apply(residual, gain_attn_full).astype(jnp.bfloat16)
    attn_pre = jnp.dot(normed, attn_full, preferred_element_type=jnp.float32)
    query_pre = attn_pre[:, :query_width]
    key_pre = attn_pre[:, query_width : query_width + kv_width]
    value_pre = attn_pre[:, query_width + kv_width : attn_width]
    cosine, sine = rotary_tables(positions.reshape(tokens_here), head_dim)
    cosine = cosine[:, None, :]
    sine = sine[:, None, :]
    query_heads = query_pre.reshape(tokens_here, heads_query, head_dim)
    key_heads = key_pre.reshape(tokens_here, heads_kv, head_dim)
    gain_q = gain_query.astype(jnp.float32)
    gain_k = gain_key.astype(jnp.float32)
    query_b = rotate(rms_apply(query_heads, gain_q), cosine, sine).astype(jnp.bfloat16)
    query_b = query_b.reshape(rows_here, seg_tok, heads_kv, grouping, head_dim)
    key_b = rotate(rms_apply(key_heads, gain_k), cosine, sine).astype(jnp.bfloat16)
    key_b = key_b.reshape(rows_here, seg_tok, kv_width)
    value_b = value_pre.astype(jnp.bfloat16).reshape(rows_here, seg_tok, kv_width)
    kv_all = ring_gather(jnp.concatenate([key_b, value_b], axis=2), 1, 0)
    keys_all = kv_all[:, :, :kv_width]
    values_all = kv_all[:, :, kv_width:]
    seg_query = segment_ids.astype(jnp.float32)
    query_spots = seq_place * seg_tok + jnp.arange(seg_tok, dtype=jnp.int32)
    stat_shape = (rows_here, heads_kv, grouping, seg_tok)

    def block_keys(block_start):
        keys_blk = lax.dynamic_slice_in_dim(keys_all, block_start, key_block, 1)
        values_blk = lax.dynamic_slice_in_dim(values_all, block_start, key_block, 1)
        shape_blk = (rows_here, key_block, heads_kv, head_dim)
        return (keys_blk.reshape(shape_blk), values_blk.reshape(shape_blk))

    def block_scores(block_start, keys_blk):
        scores = (
            jnp.einsum("rqhgd,rkhd->rhgqk", query_b, keys_blk, preferred_element_type=jnp.float32)
            * score_scale
        )
        key_spots = block_start + jnp.arange(key_block, dtype=jnp.int32)
        seg_blk = lax.dynamic_slice_in_dim(seg_keys, block_start, key_block, 1).astype(jnp.float32)
        allowed = (key_spots[None, None, :] <= query_spots[None, :, None]) & (
            seg_blk[:, None, :] == seg_query[:, :, None]
        )
        return jnp.where(allowed[:, None, None], scores, masked_score)

    def stats_step(block_index, state_in):
        running_max, running_sum = state_in
        block_start = block_index * key_block
        keys_blk, values_blk = block_keys(block_start)
        scores = block_scores(block_start, keys_blk)
        new_max = jnp.maximum(running_max, jnp.max(scores, axis=-1))
        running_sum = running_sum * jnp.exp(running_max - new_max) + jnp.sum(
            jnp.exp(scores - new_max[..., None]), axis=-1
        )
        return (new_max, running_sum)

    running_max, running_sum = lax.fori_loop(
        0,
        block_total,
        stats_step,
        (jnp.full(stat_shape, masked_score, jnp.float32), jnp.zeros(stat_shape, jnp.float32)),
    )
    log_total = running_max + jnp.log(running_sum)

    def output_step(block_index, accum_in):
        block_start = block_index * key_block
        keys_blk, values_blk = block_keys(block_start)
        prob_blk = jnp.exp(block_scores(block_start, keys_blk) - log_total[..., None]).astype(
            jnp.bfloat16
        )
        return accum_in + jnp.einsum(
            "rhgqk,rkhd->rqhgd", prob_blk, values_blk, preferred_element_type=jnp.float32
        )

    attended = lax.fori_loop(
        0,
        block_total,
        output_step,
        jnp.zeros((rows_here, seg_tok, heads_kv, grouping, head_dim), jnp.float32),
    )
    attended_b = attended.reshape(tokens_here, heads_query * head_dim).astype(jnp.bfloat16)
    middle = residual + jnp.dot(attended_b, out_full, preferred_element_type=jnp.float32)
    ffn_in = rms_apply(middle, gain_ffn_full).astype(jnp.bfloat16)
    ffn_all = jnp.concatenate(rows_gather(ffn_in), axis=0)
    gate_val = jnp.dot(ffn_all, gate_loc, preferred_element_type=jnp.float32)
    up_val = jnp.dot(ffn_all, up_loc, preferred_element_type=jnp.float32)
    hidden_b = (jax.nn.silu(gate_val) * up_val).astype(jnp.bfloat16)
    down_terms = jnp.dot(hidden_b, down_loc, preferred_element_type=jnp.float32)
    down_mine = rows_scatter(jnp.split(down_terms.astype(jnp.bfloat16), 4, axis=0))
    output = middle + down_mine
    output_b = output.astype(jnp.bfloat16).reshape(rows_here, seg_tok, feature_count)
    grad_hidden = times_transposed(cot_all, down_loc)
    grad_down_w = transposed_times(hidden_b, cot_all)
    sigma_gate = jax.nn.sigmoid(gate_val)
    grad_gate_b = (
        grad_hidden * up_val * sigma_gate * (1.0 + gate_val * (1.0 - sigma_gate))
    ).astype(jnp.bfloat16)
    grad_up_b = (grad_hidden * gate_val * sigma_gate).astype(jnp.bfloat16)
    ffn_in_terms = times_transposed(grad_gate_b, gate_loc) + times_transposed(grad_up_b, up_loc)
    grad_gate_w = transposed_times(ffn_all, grad_gate_b)
    grad_up_w = transposed_times(ffn_all, grad_up_b)
    grad_ffn_in = rows_scatter(jnp.split(ffn_in_terms.astype(jnp.bfloat16), 4, axis=0))
    ffn_sums = (
        ring_scatter(grad_gate_w.astype(jnp.bfloat16), 0, 0),
        ring_scatter(grad_up_w.astype(jnp.bfloat16), 0, 0),
        ring_scatter(grad_down_w.astype(jnp.bfloat16), 1, 0),
    )
    grad_mid_ffn, gain_ffn_rows = rms_back(middle, gain_ffn_full, grad_ffn_in)
    grad_middle = grad_top_b.astype(jnp.float32) + grad_mid_ffn
    grad_gain_ffn = jnp.sum(gain_ffn_rows, axis=0)
    grad_branch = grad_middle.astype(jnp.bfloat16)
    branch_all = jnp.concatenate(rows_gather(grad_branch), axis=0)
    grad_out_w = ring_scatter(
        transposed_times(rows_exchange(attended_b), branch_all).astype(jnp.bfloat16), 0, 1
    )
    grad_attended = times_transposed(grad_branch, out_full).astype(jnp.bfloat16)
    grad_att = grad_attended.reshape(rows_here, seg_tok, heads_kv, grouping, head_dim)

    def delta_step(block_index, accum_in):
        block_start = block_index * key_block
        keys_blk, values_blk = block_keys(block_start)
        prob_blk = jnp.exp(block_scores(block_start, keys_blk) - log_total[..., None])
        grad_probs = jnp.einsum(
            "rqhgd,rkhd->rhgqk", grad_att, values_blk, preferred_element_type=jnp.float32
        )
        return accum_in + jnp.sum(prob_blk * grad_probs, axis=-1)

    delta_row = lax.fori_loop(0, block_total, delta_step, jnp.zeros(stat_shape, jnp.float32))
    kv_shape = (rows_here, row_len, heads_kv, head_dim)

    def grad_step(block_index, state_in):
        grad_query_acc, grad_keys_acc, grad_values_acc = state_in
        block_start = block_index * key_block
        keys_blk, values_blk = block_keys(block_start)
        prob_blk = jnp.exp(block_scores(block_start, keys_blk) - log_total[..., None])
        grad_probs = jnp.einsum(
            "rqhgd,rkhd->rhgqk", grad_att, values_blk, preferred_element_type=jnp.float32
        )
        grad_scores = (prob_blk * (grad_probs - delta_row[..., None])).astype(jnp.bfloat16)
        grad_query_acc = (
            grad_query_acc
            + jnp.einsum(
                "rhgqk,rkhd->rqhgd", grad_scores, keys_blk, preferred_element_type=jnp.float32
            )
            * score_scale
        )
        key_part = (
            jnp.einsum(
                "rhgqk,rqhgd->rkhd", grad_scores, query_b, preferred_element_type=jnp.float32
            )
            * score_scale
        )
        value_part = jnp.einsum(
            "rhgqk,rqhgd->rkhd",
            prob_blk.astype(jnp.bfloat16),
            grad_att,
            preferred_element_type=jnp.float32,
        )
        grad_keys_acc = lax.dynamic_update_slice_in_dim(grad_keys_acc, key_part, block_start, 1)
        grad_values_acc = lax.dynamic_update_slice_in_dim(
            grad_values_acc, value_part, block_start, 1
        )
        return (grad_query_acc, grad_keys_acc, grad_values_acc)

    grad_query_rot, grad_keys_full, grad_values_full = lax.fori_loop(
        0,
        block_total,
        grad_step,
        (
            jnp.zeros((rows_here, seg_tok, heads_kv, grouping, head_dim), jnp.float32),
            jnp.zeros(kv_shape, jnp.float32),
            jnp.zeros(kv_shape, jnp.float32),
        ),
    )
    kv_grads = jnp.concatenate(
        [
            grad_keys_full.reshape(rows_here, row_len, kv_width),
            grad_values_full.reshape(rows_here, row_len, kv_width),
        ],
        axis=2,
    ).astype(jnp.bfloat16)
    kv_mine = ring_scatter(kv_grads, 1, 0)
    grad_keys_mine = kv_mine[:, :, :kv_width]
    grad_values_mine = kv_mine[:, :, kv_width:]
    grad_value_b = grad_values_mine.reshape(tokens_here, heads_kv * head_dim).astype(jnp.bfloat16)
    grad_key_norm = rotate_back(
        grad_keys_mine.reshape(tokens_here, heads_kv, head_dim), cosine, sine
    )
    grad_key_pre, gain_k_rows = rms_back(key_heads, gain_k, grad_key_norm)
    grad_key_b = grad_key_pre.reshape(tokens_here, heads_kv * head_dim).astype(jnp.bfloat16)
    grad_query_norm = rotate_back(
        grad_query_rot.reshape(tokens_here, heads_query, head_dim), cosine, sine
    )
    grad_query_pre, gain_q_rows = rms_back(query_heads, gain_q, grad_query_norm)
    grad_query_b = grad_query_pre.reshape(tokens_here, heads_query * head_dim).astype(jnp.bfloat16)
    normed_share = rows_exchange(normed)
    query_grads = jnp.concatenate(rows_gather(grad_query_b), axis=0)
    grad_kv_b = jnp.concatenate([grad_key_b, grad_value_b], axis=1)
    kv_grads_all = jnp.concatenate(rows_gather(grad_kv_b), axis=0)
    grad_query_w = ring_scatter(
        transposed_times(normed_share, query_grads).astype(jnp.bfloat16), 0, 0
    )
    grad_kv_w = ring_scatter(
        transposed_times(normed_share, kv_grads_all).astype(jnp.bfloat16), 0, 0
    )
    grad_normed = times_transposed(
        jnp.concatenate([grad_query_b, grad_kv_b], axis=1), attn_full[:, :attn_width]
    )
    grad_resid_attn, gain_attn_rows = rms_back(residual, gain_attn_full, grad_normed)
    grad_inputs = (grad_middle + grad_resid_attn).reshape(rows_here, seg_tok, feature_count)
    gain_parts = jnp.concatenate(
        [
            jnp.sum(gain_attn_rows, axis=0),
            grad_gain_ffn,
            jnp.sum(gain_q_rows, axis=(0, 1)),
            jnp.sum(gain_k_rows, axis=(0, 1)),
        ]
    )
    part_size = gain_parts.shape[0]
    gain_parts = jnp.pad(gain_parts, (0, -part_size % 1024)).reshape(8, -1)
    gain_all = lax.all_gather(gain_parts, ("rows", "seq"), axis=0, tiled=False)
    gain_sums = jnp.sum(gain_all, axis=0).reshape(-1)
    share_start = (lax.axis_index("rows") * lax.axis_size("seq") + seq_place) * feature_share
    head_start = 2 * feature_count
    return (
        output_b,
        grad_inputs,
        grad_query_w,
        grad_kv_w[:, :kv_width],
        grad_kv_w[:, kv_width:],
        grad_out_w,
        ffn_sums[0],
        ffn_sums[1],
        ffn_sums[2],
        lax.dynamic_slice_in_dim(gain_sums, share_start, feature_share),
        gain_sums[head_start : head_start + head_dim],
        gain_sums[head_start + head_dim : head_start + 2 * head_dim],
        lax.dynamic_slice_in_dim(gain_sums, feature_count + share_start, feature_share),
    )


def solution(mesh):
    return jax.shard_map(
        local,
        mesh=mesh,
        in_specs=(
            P("rows", "seq", None),
            P("rows", "seq", None),
            P("rows", "seq"),
            P("rows", "seq"),
            P(("rows", "seq"), None),
            P(("rows", "seq"), None),
            P(("rows", "seq"), None),
            P(("rows", "seq"), None),
            P("seq", "rows"),
            P("seq", "rows"),
            P("rows", "seq"),
            P(("rows", "seq")),
            P(),
            P(),
            P(("rows", "seq")),
        ),
        out_specs=(
            P("rows", "seq", None),
            P("rows", "seq", None),
            P(("rows", "seq"), None),
            P(("rows", "seq"), None),
            P(("rows", "seq"), None),
            P(("rows", "seq"), None),
            P("seq", "rows"),
            P("seq", "rows"),
            P("rows", "seq"),
            P(("rows", "seq")),
            P(),
            P(),
            P(("rows", "seq")),
        ),
        check_vma=False,
    )
```
